32 devices in a mesh: groups: 2 (over x), row: 2 (over core), col: 8 (over z, y).
Axes of the slice: x: 2, y: 2, z: 4, core: 2. Of those that a mesh axis runs over, the one named last changes fastest.
Arguments:
- slab: float32 [5120, 28672], P(('groups', 'row'), 'col'), parts along dimension 0, as said below
- pivots: int32 [8, 512], P('groups'), parts along dimension 0, may hold values from 0 to 2559, as said below
Outputs:
- pruned: float32 [5120, 28672], P(('groups', 'row'), 'col'), parts along dimension 0
The draws below stay inside these ranges and needn't reach their ends.
There are 2 independent parts, one for each index of `groups`. The reference program is written for one: setup_inputs(seed, part) draws one part's arguments, and reference() takes and returns one part's arrays. A program takes and returns all parts, laid end to end along the dimension named above; each array names one. Nothing has to cross between parts.
Inputs may be any that keep to these rules, and one draw needn't show every extreme that they name: `pivots`: in every block j, list positions c * 64 to (c + 1) * 64 - 1 hold slab rows of c * 320 to (c + 1) * 320 - 1; no slab row appears twice in the whole array. slab[r, g(r')] = slab[r', g(r)] for all slab rows r, r', and the square matrix of these entries is positive definite.
All inputs are finite; a program needn't handle non-finite values.
Results may differ from the reference program's by a relative error of at most 0.00045.
Values sent between devices are 32-bit elements; how exact they have to be, the bound alone decides.
No kernel may reach another device: no remote copies, remote signals or barrier semaphores. Data moves between devices by JAX's collectives and lax.ppermute only.
A program may use at most 192 MiB of HBM per device.

```python
import jax
import jax.numpy as jnp
from jax import lax

COLS = 28672
ROWS = 2560
PIVOTS = 512
BLOCKS = 4
PIV_DEV = 64
ROW_SHARE = 320
SHARE_COLS = 3584
N_COL = 8


reach = 6.0


near_weight = 0.6


far_weight = 0.4


common_weight = 0.3


def draw_slab(key, part):
    keys = jax.random.split(jax.random.fold_in(key, 11), 6)
    places = jax.random.uniform(keys[0], (ROWS,), jnp.float32) * ROWS
    distance = jnp.abs(places[:, None] - places[None, :])
    far_reach = ROWS / 8.0
    scales = jnp.exp(jax.random.uniform(keys[1], (ROWS,), jnp.float32, -0.69, 0.69))
    others = jax.random.normal(keys[2], (ROWS, COLS), jnp.float32)
    diagonal = jax.random.uniform(keys[3], (ROWS,), jnp.float32, 0.3, 1.2)
    common = scales * jax.random.uniform(keys[5], (ROWS,), jnp.float32, 0.5, 1.5)
    kernel = near_weight * jnp.exp(-distance / reach) + far_weight * jnp.exp(-distance / far_reach)
    square = scales[:, None] * scales[None, :] * kernel
    square = square + common_weight * common[:, None] * common[None, :]
    square = square + jnp.eye(ROWS, dtype=jnp.float32) * diagonal[:, None]
    index = jnp.arange(ROWS, dtype=jnp.int32)
    where = index // ROW_SHARE * SHARE_COLS + index % ROW_SHARE
    return others.at[:, where].set(square)


def draw_pivots(key, part):
    owners = PIVOTS // PIV_DEV
    keys = jax.random.split(jax.random.fold_in(key, 23), owners)
    perms = jax.vmap(lambda k: jax.random.permutation(k, ROW_SHARE))(keys).astype(jnp.int32)
    taken = perms[:, :BLOCKS * PIV_DEV].reshape(owners, BLOCKS, PIV_DEV)
    taken = taken + (jnp.arange(owners, dtype=jnp.int32) * ROW_SHARE)[:, None, None]
    return jnp.transpose(taken, (1, 0, 2)).reshape(BLOCKS, PIVOTS)


def setup_inputs(seed: int = 0, part: int = 0) -> dict:
    streams_of = jax.random.split(jax.random.key(seed), 3)
    part_keys = jax.random.split(jax.random.fold_in(streams_of[2], part), 3)
    return {
        "slab": draw_slab(jax.random.fold_in(jax.random.fold_in(streams_of[2], part), 71), part),
        "pivots": draw_pivots(jax.random.fold_in(jax.random.fold_in(streams_of[2], part), 71), part),
    }


def invert_with(factor):
    order = factor.shape[0]
    identity = jnp.eye(order, dtype=factor.dtype)
    forward = lax.linalg.triangular_solve(factor, identity, left_side=True, lower=True)
    return lax.linalg.triangular_solve(factor, forward, left_side=True, lower=True, transpose_a=True)

def reference(slab, pivots):
    share = ROWS // N_COL
    share_cols = COLS // N_COL
    current = slab
    for block in range(BLOCKS):
        rows_idx = pivots[block].astype(jnp.int32)
        cols_idx = (rows_idx // share * share_cols + rows_idx % share).astype(jnp.int32)
        strip = current[:, cols_idx]
        panel = current[rows_idx, :]
        pivot = strip[rows_idx, :]
        factor = jnp.linalg.cholesky(pivot)
        inverse = invert_with(factor)
        solved = jnp.dot(inverse, panel, precision=lax.Precision.HIGHEST)
        current = current - jnp.dot(strip, solved, precision=lax.Precision.HIGHEST)
    return current
```

```python
import functools

import jax
import jax.numpy as jnp
from jax import lax
from jax.experimental import pallas as pl
from jax.experimental.pallas import tpu as pltpu
from jax.sharding import PartitionSpec as P

LANES = 128
SUBS = 8
HALF = jnp.bfloat16
ANY = pl.BlockSpec(memory_space=pltpu.VMEM)
SCALARS = pl.BlockSpec(memory_space=pltpu.SMEM)
VMEM_BYTES = 60 * 1024 * 1024

LEAD = (((0,), (0,)), ((), ()))
LAST = (((1,), (1,)), ((), ()))
PLAIN = (((1,), (0,)), ((), ()))


def mxu(left, right, dims):
    return lax.dot_general(left, right, dims, preferred_element_type=jnp.float32)


def two(x):
    high = x.astype(HALF)
    return high, (x - high.astype(jnp.float32)).astype(HALF)


def three(x):
    high = x.astype(HALF)
    rest = x - high.astype(jnp.float32)
    middle = rest.astype(HALF)
    return high, middle, (rest - middle.astype(jnp.float32)).astype(HALF)


def product(left, right, dims):
    return (
        mxu(left[0], right[0], dims)
        + mxu(left[0], right[1], dims)
        + mxu(left[1], right[0], dims)
    )


def over_lanes(x, lane):
    return jnp.broadcast_to(x[:, lane : lane + 1], (SUBS, LANES))


def over_subs(x, sub):
    return jnp.broadcast_to(x[sub : sub + 1, :], (SUBS, LANES))


def gram(left, right):
    lh, lm, ll = three(left)
    rh, rm, rl = three(right)
    a = jnp.concatenate([lh, lm, lh, lm, ll, lh], 0)
    b = jnp.concatenate([rh, rh, rm, rm, rh, rl], 0)
    return mxu(a, b, LEAD)


def inverse_factor(v, order):
    wide = order // LANES
    panels = order // SUBS
    lane = lax.broadcasted_iota(jnp.int32, (SUBS, LANES), 1)
    sub = lax.broadcasted_iota(jnp.int32, (SUBS, LANES), 0)

    def load(q):
        return [v[q, :, LANES * c : LANES * (c + 1)] for c in range(wide)]

    def cleared(x, block, inside):
        return [jnp.where(inside, 0.0, x[c]) if c == block else x[c] for c in range(wide)]

    here, after = load(0), load(1)
    diag = [over_lanes(here[0], j) for j in range(SUBS)]
    for p in range(panels):
        block, first = SUBS * p // LANES, SUBS * p % LANES
        inside = (lane >= first) & (lane < first + SUBS)
        rows = [[over_subs(here[c], k) for c in range(wide)] for k in range(SUBS)]
        for k in range(SUBS):
            unit = jnp.where(lane == first + k, 1.0, 0.0)
            rows[k][block] = jnp.where(inside, unit, rows[k][block])
        one, two_on = p + 1 < panels, p + 2 < panels
        if one:
            nblock, nfirst = SUBS * (p + 1) // LANES, SUBS * (p + 1) % LANES
            x1 = [over_lanes(after[block], first + k) for k in range(SUBS)]
            ndiag = [over_lanes(after[nblock], nfirst + k) for k in range(SUBS)]
            nhere = cleared(after, block, inside)
        if two_on:
            far = load(p + 2)
            x2 = [over_lanes(far[block], first + k) for k in range(SUBS)]
            nafter = cleared(far, block, inside)
        packed = [None] * wide
        for k in range(SUBS):
            pivot = over_subs(diag[k], k)
            recip = 1.0 / pivot
            scale = lax.rsqrt(pivot)
            later = range(k + 1, SUBS)
            entry = {j: over_subs(diag[k], j) for j in later}
            column = diag[k] * recip
            for j in later:
                diag[j] = diag[j] - column * entry[j]
            for j in later:
                factor = entry[j] * recip
                for c in range(wide):
                    rows[j][c] = rows[j][c] - factor * rows[k][c]
            if one:
                column = x1[k] * recip
                for j in later:
                    x1[j] = x1[j] - column * entry[j]
                for i in range(SUBS):
                    ndiag[i] = ndiag[i] - x1[k] * over_subs(column, i)
                for c in range(wide):
                    nhere[c] = nhere[c] - column * rows[k][c]
            if two_on:
                column = x2[k] * recip
                for j in later:
                    x2[j] = x2[j] - column * entry[j]
                for c in range(wide):
                    nafter[c] = nafter[c] - column * rows[k][c]
            for c in range(wide):
                row = rows[k][c] * scale
                packed[c] = row if k == 0 else jnp.where(sub == k, row, packed[c])
        for c in range(wide):
            v[p, :, LANES * c : LANES * (c + 1)] = packed[c]
        if one:
            diag, here = ndiag, nhere
        if two_on:
            after = nafter
        if p + 3 < panels:
            start = SUBS * (p + 3) // LANES
            change = gram(jnp.concatenate(packed[start:], 1), jnp.concatenate(packed, 1))
            for q in range(p + 3, panels):
                at = SUBS * q - LANES * start
                for c in range(wide):
                    old = v[q, :, LANES * c : LANES * (c + 1)]
                    if c == block:
                        old = jnp.where(inside, 0.0, old)
                    new = change[at : at + SUBS, LANES * c : LANES * (c + 1)]
                    v[q, :, LANES * c : LANES * (c + 1)] = old - new


def params():
    return pltpu.CompilerParams(vmem_limit_bytes=VMEM_BYTES)


def prepare_kernel(blocks, per, kept_here, slab_ref, own_ref, rows_ref, *outs):
    rows_here, width = slab_ref.shape
    picks = own_ref.shape[0]
    listed = rows_ref.shape[0]
    kept_ref, where_ref = outs[blocks], outs[blocks + 1]
    f32 = jnp.float32
    column = lax.broadcasted_iota(jnp.int32, (picks, width), 1)
    choose = jnp.where(own_ref[...] == column, 1.0, 0.0).astype(HALF)
    row = lax.broadcasted_iota(jnp.int32, (listed, rows_here), 1)
    hit = jnp.where(rows_ref[...] == row, 1.0, 0.0)
    kept = 1.0 - jnp.sum(hit, axis=0, keepdims=True)
    before = lax.broadcasted_iota(jnp.int32, (rows_here, rows_here), 0) < (
        lax.broadcasted_iota(jnp.int32, (rows_here, rows_here), 1)
    )
    before = jnp.where(before, 1.0, 0.0).astype(HALF)
    rank = mxu(jnp.broadcast_to(kept, (SUBS, rows_here)).astype(HALF), before, PLAIN)
    place = lax.broadcasted_iota(jnp.int32, (kept_here, rows_here), 0).astype(f32)
    hit_kept = jnp.where((rank[0:1, :] == place) & (kept > 0.5), 1.0, 0.0)
    number = lax.broadcasted_iota(jnp.int32, (kept_here, rows_here), 1).astype(f32)
    kept_ref[...] = hit_kept.astype(HALF)
    where_ref[...] = jnp.broadcast_to(
        jnp.sum(hit_kept * number, axis=1, keepdims=True), where_ref.shape
    ).astype(jnp.int32)
    order = jnp.concatenate([hit.astype(HALF), hit_kept.astype(HALF)], 0)
    total = None
    for piece in three(slab_ref[...]):
        chosen = mxu(choose, piece, LAST).astype(HALF)
        part = mxu(chosen, order, LAST)
        total = part if total is None else total + part
    for t in range(blocks):
        outs[t][...] = total[per * t : per * (t + 1), LANES * t :]


def prepare(slab, own, rows, blocks, per, kept_here, share):
    rows_here = slab.shape[0]
    width = -(-share // LANES) * LANES
    listed = rows.shape[0]
    shapes = [
        jax.ShapeDtypeStruct((per, listed - LANES * t + kept_here), jnp.float32)
        for t in range(blocks)
    ]
    shapes.append(jax.ShapeDtypeStruct((kept_here, rows_here), HALF))
    shapes.append(jax.ShapeDtypeStruct((kept_here, LANES), jnp.int32))
    return pl.pallas_call(
        functools.partial(prepare_kernel, blocks, per, kept_here),
        grid=(1,),
        in_specs=[
            pl.BlockSpec((rows_here, width), lambda i: (0, 0)),
            pl.BlockSpec(own.shape, lambda i: (0, 0)),
            pl.BlockSpec(rows.shape, lambda i: (0, 0)),
        ],
        out_specs=[pl.BlockSpec(s.shape, lambda i: (0, 0)) for s in shapes],
        out_shape=shapes,
        compiler_params=params(),
        name="prepare",
    )(slab, own, rows)


def reversed_bits(x, count):
    out = jnp.int32(0)
    for bit in range(count):
        out = out | (((x >> bit) & 1) << (count - 1 - bit))
    return out


def factor_kernel(t, size, here_ref, own_ref, other_ref, *refs):
    past = [(refs[2 * i], refs[2 * i + 1]) for i in range(t)]
    high_ref, low_ref, current, v = refs[2 * t :]
    n_col, per, lanes = own_ref.shape
    paired = other_ref.shape[2]
    bits = n_col.bit_length() - 1
    col, row = here_ref[0], here_ref[1]
    for c in range(n_col):
        at = reversed_bits(c ^ col, bits)
        rows = slice(per * c, per * (c + 1))
        for k in range(paired // LANES):
            part = slice(LANES * k, LANES * (k + 1))
            base = 2 * LANES * k
            mine = pl.ds(pl.multiple_of(base + row * LANES, LANES), LANES)
            others = pl.ds(pl.multiple_of(base + (1 - row) * LANES, LANES), LANES)
            current[rows, mine] = own_ref[at, :, part]
            current[rows, others] = other_ref[at, :, part]
        current[rows, 2 * paired :] = own_ref[at, :, paired:]
    width = current.shape[1]
    for start in range(0, width, size):
        total = current[:, start : start + size]
        for i in range(t):
            off = (t - i) * size
            left = [ref[:, off : off + size] for ref in past[i]]
            right = [ref[:, off + start : off + start + size] for ref in past[i]]
            total = total - product(left, right, LEAD)
        current[:, start : start + size] = total
    v[...] = current[:, :size].reshape(size // SUBS, SUBS, size)
    inverse_factor(v, size)
    down = lax.broadcasted_iota(jnp.int32, (size, size), 0)
    across = lax.broadcasted_iota(jnp.int32, (size, size), 1)
    inverse = two(jnp.where(across <= down, v[...].reshape(size, size), 0.0))
    high_ref[:, :size], low_ref[:, :size] = inverse
    for start in range(size, width, size):
        part = slice(start, start + size)
        high_ref[:, part], low_ref[:, part] = two(
            product(inverse, two(current[:, part]), PLAIN)
        )


def factor(t, size, here, own, other, past):
    width = 2 * other.shape[2] + own.shape[2] - other.shape[2]
    flat = [x for pair in past for x in pair]
    shape = jax.ShapeDtypeStruct((size, width), HALF)
    return pl.pallas_call(
        functools.partial(factor_kernel, t, size),
        in_specs=[SCALARS] + [ANY] * (2 + len(flat)),
        out_specs=[ANY, ANY],
        out_shape=[shape, shape],
        scratch_shapes=[
            pltpu.VMEM((size, width), jnp.float32),
            pltpu.VMEM((size // SUBS, SUBS, size), jnp.float32),
        ],
        compiler_params=params(),
        cost_estimate=pl.CostEstimate(
            flops=20_000_000_000, bytes_accessed=20_000_000, transcendentals=0
        ),
        name="factor",
    )(here, own, other, *flat)


def back_kernel(count, size, kept_here, here_ref, kept_ref, mine_ref, theirs_ref, *refs):
    past = [(refs[2 * i], refs[2 * i + 1]) for i in range(count)]
    out_high, out_low, wh, wl = refs[2 * count :]
    row = here_ref[1]
    f32 = jnp.float32
    for t in reversed(range(count)):
        high, low = past[t]
        end = (count - t) * size
        z = high[:, end:].astype(f32) + low[:, end:].astype(f32)
        if t + 1 < count:
            left = (high[:, size:end], low[:, size:end])
            later = slice((t + 1) * size, count * size)
            z = z - product(left, (wh[later, :], wl[later, :]), PLAIN)
        w = product((high[:, :size], low[:, :size]), two(z), LEAD)
        rows = slice(t * size, (t + 1) * size)
        wh[rows, :], wl[rows, :] = two(w)
    rows_here = kept_ref.shape[1]
    half = size // 2
    for side, rows_ref in ((0, mine_ref), (1, theirs_ref)):
        from_row = row if side == 0 else 1 - row
        listed = rows_ref.shape[0]
        number = lax.broadcasted_iota(jnp.int32, (listed, rows_here), 1)
        hit = jnp.where(rows_ref[...] == number, 1.0, 0.0).astype(HALF)
        for out, w in ((out_high, wh), (out_low, wl)):
            picked = jnp.concatenate(
                [
                    w[pl.ds(pl.multiple_of(t * size + from_row * half, half), half), :]
                    for t in range(count)
                ],
                0,
            )
            spread = -mxu(picked, hit, LEAD)
            if side == 0 and out is out_high:
                spread = spread + kept_ref[...].astype(f32)
            out[:, side * rows_here : (side + 1) * rows_here] = spread.astype(HALF)


def back(size, kept_here, here, kept, mine, theirs, past):
    rows_here = kept.shape[1]
    flat = [x for pair in past for x in pair]
    shape = jax.ShapeDtypeStruct((kept_here, 2 * rows_here), HALF)
    count = len(past)
    return pl.pallas_call(
        functools.partial(back_kernel, count, size, kept_here),
        in_specs=[SCALARS] + [ANY] * (3 + len(flat)),
        out_specs=[ANY, ANY],
        out_shape=[shape, shape],
        scratch_shapes=[pltpu.VMEM((count * size, kept_here), HALF)] * 2,
        compiler_params=params(),
        cost_estimate=pl.CostEstimate(
            flops=20_000_000_000, bytes_accessed=20_000_000, transcendentals=0
        ),
        name="back",
    )(here, kept, mine, theirs, *flat)


def final_kernel(where_ref, high_ref, low_ref, mine_ref, theirs_ref, out_ref, result):
    rows_here = mine_ref.shape[0]
    total = None
    for side, ref in ((0, mine_ref), (1, theirs_ref)):
        part = slice(side * rows_here, (side + 1) * rows_here)
        term = product(
            (high_ref[:, part], low_ref[:, part]), two(ref[...]), PLAIN
        )
        total = term if total is None else total + term
    result[...] = total
    out_ref[...] = jnp.zeros_like(out_ref)
    kept_here = result.shape[0]

    def store(step, carry):
        base = pl.multiple_of(step * SUBS, SUBS)
        group = result[pl.ds(base, SUBS), :]
        for k in range(SUBS):
            out_ref[pl.ds(where_ref[base + k], 1), :] = group[k : k + 1, :]
        return carry

    lax.fori_loop(0, kept_here // SUBS, store, 0)


def final(where, high, low, mine, theirs):
    rows_here, cols = mine.shape
    tile = 512
    kept_here = high.shape[0]
    whole = pl.BlockSpec(high.shape, lambda i, w: (0, 0))
    strip = pl.BlockSpec((rows_here, tile), lambda i, w: (0, i))
    return pl.pallas_call(
        final_kernel,
        grid_spec=pltpu.PrefetchScalarGridSpec(
            num_scalar_prefetch=1,
            grid=(cols // tile,),
            in_specs=[whole, whole, strip, strip],
            out_specs=strip,
            scratch_shapes=[pltpu.VMEM((kept_here, tile), jnp.float32)],
        ),
        out_shape=jax.ShapeDtypeStruct((rows_here, cols), jnp.float32),
        compiler_params=params(),
        name="final",
    )(where, high, low, mine, theirs)


def per_device(slab, pivots):
    rows_here = slab.shape[0]
    n_col = lax.axis_size("col")
    n_row = lax.axis_size("row")
    col = lax.axis_index("col")
    row = lax.axis_index("row")
    lists, total = pivots.shape
    size = 256
    per = size // n_col
    pieces = total // size
    count = lists * pieces
    share = rows_here * n_row // n_col
    kept_here = rows_here - lists * total // n_row

    listed = pivots.reshape(lists, n_col, pieces, per)
    listed = jnp.transpose(listed, (0, 2, 1, 3)).reshape(count, n_col, per)
    own = lax.dynamic_index_in_dim(listed, col, 1, keepdims=False) - col * share
    own = own.reshape(count * per, 1)
    by_row = listed.reshape(count, n_row, size // n_row)
    mine = lax.dynamic_index_in_dim(by_row, row, 1, keepdims=False) - row * rows_here
    theirs = (
        lax.dynamic_index_in_dim(by_row, 1 - row, 1, keepdims=False)
        - (1 - row) * rows_here
    )
    mine = mine.reshape(-1, 1)
    theirs = theirs.reshape(-1, 1)
    here = jnp.stack([col, row]).astype(jnp.int32)

    swap = [(0, 1), (1, 0)]
    other_slab = lax.ppermute(slab, "row", swap)
    prepared = prepare(slab, own, mine, count, per, kept_here, share)
    kept, where = prepared[count], prepared[count + 1]

    def gathered(t):
        held = prepared[t][None]
        bit = n_col // 2
        while bit:
            pairs = [(c, c ^ bit) for c in range(n_col)]
            held = jnp.concatenate([held, lax.ppermute(held, "col", pairs)], 0)
            bit //= 2
        paired = held.shape[2] - kept_here
        return held, lax.ppermute(held[:, :, :paired], "row", swap)

    past = []
    for t in range(count):
        held, others = gathered(t)
        past.append(factor(t, size, here, held, others, past))
    high, low = back(size, kept_here, here, kept, mine, theirs, past)
    return final(where[:, 0], high, low, slab, other_slab)


def solution(mesh):
    in_specs = (P(("groups", "row"), "col"), P("groups", None))
    out_specs = P(("groups", "row"), "col")
    return jax.shard_map(
        per_device, mesh=mesh, in_specs=in_specs, out_specs=out_specs, check_vma=False
    )
```

```python
import functools

import jax
import jax.numpy as jnp
from jax import lax
from jax.experimental import pallas as pl
from jax.experimental.pallas import tpu as pltpu
from jax.sharding import PartitionSpec as P

LANES = 128
SUBS = 8
HALF = jnp.bfloat16
ANY = pl.BlockSpec(memory_space=pltpu.VMEM)
SCALARS = pl.BlockSpec(memory_space=pltpu.SMEM)
AHEAD = 3
VMEM_BYTES = 60 * 1024 * 1024

LEAD = (((0,), (0,)), ((), ()))
LAST = (((1,), (1,)), ((), ()))
PLAIN = (((1,), (0,)), ((), ()))


def mxu(left, right, dims):
    return lax.dot_general(left, right, dims, preferred_element_type=jnp.float32)


def two(x):
    high = x.astype(HALF)
    return high, (x - high.astype(jnp.float32)).astype(HALF)


def three(x):
    high = x.astype(HALF)
    rest = x - high.astype(jnp.float32)
    middle = rest.astype(HALF)
    return high, middle, (rest - middle.astype(jnp.float32)).astype(HALF)


def product(left, right, dims):
    rows = left[0].shape[0]
    both = mxu(jnp.concatenate(left, 0), right[0], dims)
    return both[:rows] + both[rows:] + mxu(left[0], right[1], dims)


def over_lanes(x, lane):
    return jnp.broadcast_to(x[:, lane : lane + 1], (SUBS, LANES))


def over_subs(x, sub):
    return jnp.broadcast_to(x[sub : sub + 1, :], (SUBS, LANES))


def gram(left, right):
    lh, lm, ll = three(left)
    rh, rm, rl = three(right)
    a = jnp.concatenate([lh, lm, lh, lm, ll, lh], 0)
    b = jnp.concatenate([rh, rh, rm, rm, rh, rl], 0)
    return mxu(a, b, LEAD)


def inverse_factor(v, order):
    wide = order // LANES
    panels = order // SUBS
    lane = lax.broadcasted_iota(jnp.int32, (SUBS, LANES), 1)
    sub = lax.broadcasted_iota(jnp.int32, (SUBS, LANES), 0)

    def load(q):
        return [v[q, :, LANES * c : LANES * (c + 1)] for c in range(wide)]

    def cleared(x, block, inside):
        return [jnp.where(inside, 0.0, x[c]) if c == block else x[c] for c in range(wide)]

    held = [load(q) for q in range(min(AHEAD, panels))]
    diag = [over_lanes(held[0][0], j) for j in range(SUBS)]
    for p in range(panels):
        block, first = SUBS * p // LANES, SUBS * p % LANES
        inside = (lane >= first) & (lane < first + SUBS)
        here = held[0]
        rows = [[over_subs(here[c], k) for c in range(wide)] for k in range(SUBS)]
        for k in range(SUBS):
            unit = jnp.where(lane == first + k, 1.0, 0.0)
            rows[k][block] = jnp.where(inside, unit, rows[k][block])
        coming = held[1:] + ([load(p + AHEAD)] if p + AHEAD < panels else [])
        entries = [[over_lanes(x[block], first + k) for k in range(SUBS)] for x in coming]
        if coming:
            nblock, nfirst = SUBS * (p + 1) // LANES, SUBS * (p + 1) % LANES
            ndiag = [over_lanes(coming[0][nblock], nfirst + k) for k in range(SUBS)]
        coming = [cleared(x, block, inside) for x in coming]
        packed = [None] * wide
        for k in range(SUBS):
            pivot = over_subs(diag[k], k)
            recip = 1.0 / pivot
            scale = lax.rsqrt(pivot)
            later = range(k + 1, SUBS)
            entry = {j: over_subs(diag[k], j) for j in later}
            column = diag[k] * recip
            for j in later:
                diag[j] = diag[j] - column * entry[j]
            for j in later:
                factor = entry[j] * recip
                for c in range(wide):
                    rows[j][c] = rows[j][c] - factor * rows[k][c]
            for a, (x, row) in enumerate(zip(entries, coming)):
                column = x[k] * recip
                for j in later:
                    x[j] = x[j] - column * entry[j]
                if a == 0:
                    for i in range(SUBS):
                        ndiag[i] = ndiag[i] - x[k] * over_subs(column, i)
                for c in range(wide):
                    row[c] = row[c] - column * rows[k][c]
            for c in range(wide):
                row = rows[k][c] * scale
                packed[c] = row if k == 0 else jnp.where(sub == k, row, packed[c])
        for c in range(wide):
            v[p, :, LANES * c : LANES * (c + 1)] = packed[c]
        if coming:
            diag, held = ndiag, coming
        if p + AHEAD + 1 < panels:
            start = SUBS * (p + AHEAD + 1) // LANES
            change = gram(jnp.concatenate(packed[start:], 1), jnp.concatenate(packed, 1))
            for q in range(p + AHEAD + 1, panels):
                at = SUBS * q - LANES * start
                for c in range(wide):
                    old = v[q, :, LANES * c : LANES * (c + 1)]
                    if c == block:
                        old = jnp.where(inside, 0.0, old)
                    new = change[at : at + SUBS, LANES * c : LANES * (c + 1)]
                    v[q, :, LANES * c : LANES * (c + 1)] = old - new


def params():
    return pltpu.CompilerParams(vmem_limit_bytes=VMEM_BYTES)


def estimate(microseconds):
    return pl.CostEstimate(
        flops=microseconds * 1_000_000_000, bytes_accessed=1_000_000, transcendentals=0
    )


def exact(left, right, dims):
    return lax.dot_general(
        left,
        right,
        dims,
        precision=lax.Precision.HIGHEST,
        preferred_element_type=jnp.float32,
    )


def inverse_of(square, v, high_ref, low_ref):
    n = LANES
    v[0] = square[:n, :n].reshape(n // SUBS, SUBS, n)
    above = square[:n, n:]
    last = square[n:, n:]
    down = lax.broadcasted_iota(jnp.int32, (n, n), 0)
    across = lax.broadcasted_iota(jnp.int32, (n, n), 1)

    def half(h, carry):
        inverse_factor(v.at[h], n)
        done = jnp.where(across <= down, v[h].reshape(n, n), 0.0)
        v[h] = done.reshape(n // SUBS, SUBS, n)

        @pl.when(h == 0)
        def _():
            upper = exact(done, above, PLAIN)
            v[2] = upper.reshape(n // SUBS, SUBS, n)
            v[1] = (last - exact(upper, upper, LEAD)).reshape(n // SUBS, SUBS, n)

        return carry

    lax.fori_loop(0, 2, half, 0)
    first, second, upper = (v[h].reshape(n, n) for h in range(3))
    corner = -exact(second, exact(upper, first, LEAD), PLAIN)
    zero = jnp.zeros((n, n), HALF)
    for at, piece in (((0, 0), first), ((n, 0), corner), ((n, n), second)):
        block = (slice(at[0], at[0] + n), slice(at[1], at[1] + n))
        high_ref[block], low_ref[block] = two(piece)
    high_ref[:n, n:] = zero
    low_ref[:n, n:] = zero


def prepare_kernel(chunks, per, kept_here, slab_ref, own_ref, rows_ref, *outs):
    rows_here, width = slab_ref.shape
    picks = own_ref.shape[0]
    listed = rows_ref.shape[0]
    pieces, (kept_ref, where_ref, hit_ref) = outs[:-3], outs[-3:]
    f32 = jnp.float32
    column = lax.broadcasted_iota(jnp.int32, (picks, width), 1)
    choose = jnp.where(own_ref[...] == column, 1.0, 0.0).astype(HALF)
    row = lax.broadcasted_iota(jnp.int32, (listed, rows_here), 1)
    hit = jnp.where(rows_ref[...] == row, 1.0, 0.0)
    kept = 1.0 - jnp.sum(hit, axis=0, keepdims=True)
    hit = hit.astype(HALF)
    hit_ref[...] = hit
    before = lax.broadcasted_iota(jnp.int32, (rows_here, rows_here), 0) < (
        lax.broadcasted_iota(jnp.int32, (rows_here, rows_here), 1)
    )
    before = jnp.where(before, 1.0, 0.0).astype(HALF)
    rank = mxu(jnp.broadcast_to(kept, (SUBS, rows_here)).astype(HALF), before, PLAIN)
    place = lax.broadcasted_iota(jnp.int32, (kept_here, rows_here), 0).astype(f32)
    hit_kept = jnp.where((rank[0:1, :] == place) & (kept > 0.5), 1.0, 0.0)
    number = lax.broadcasted_iota(jnp.int32, (kept_here, rows_here), 1).astype(f32)
    where_ref[...] = jnp.broadcast_to(
        jnp.sum(hit_kept * number, axis=1, keepdims=True), where_ref.shape
    ).astype(jnp.int32)
    hit_kept = hit_kept.astype(HALF)
    kept_ref[...] = hit_kept
    order = jnp.concatenate([hit, hit_kept], 0)
    total = None
    for piece in three(slab_ref[...]):
        chosen = mxu(choose, piece, LAST).astype(HALF)
        part = mxu(chosen, order, LAST)
        total = part if total is None else total + part
    for out, chunk in zip(pieces, chunks):
        at = 0
        for t, start, end in chunk:
            wide = LANES * (end - start)
            out[:, at : at + wide] = total[
                per * t : per * (t + 1), LANES * start : LANES * end
            ]
            at += wide


def prepare(slab, own, rows, chunks, per, kept_here, share):
    rows_here = slab.shape[0]
    width = -(-share // LANES) * LANES
    f32 = jnp.float32
    shapes = [
        jax.ShapeDtypeStruct((per, LANES * sum(e - s for _, s, e in chunk)), f32)
        for chunk in chunks
    ]
    shapes.append(jax.ShapeDtypeStruct((kept_here, rows_here), HALF))
    shapes.append(jax.ShapeDtypeStruct((kept_here, LANES), jnp.int32))
    shapes.append(jax.ShapeDtypeStruct((rows.shape[0], rows_here), HALF))
    return pl.pallas_call(
        functools.partial(prepare_kernel, chunks, per, kept_here),
        grid=(1,),
        in_specs=[
            pl.BlockSpec((rows_here, width), lambda i: (0, 0)),
            pl.BlockSpec(own.shape, lambda i: (0, 0)),
            pl.BlockSpec(rows.shape, lambda i: (0, 0)),
        ],
        out_specs=[pl.BlockSpec(s.shape, lambda i: (0, 0)) for s in shapes],
        out_shape=shapes,
        compiler_params=params(),
        cost_estimate=estimate(7),
        name="prepare",
    )(slab, own, rows)


def place_of(flipped, n_col):
    return (flipped & 1) * (n_col // 2) + (flipped >> 1)


def assemble(here_ref, own_ref, other_ref, unit, out, lane):
    n_col, per, _ = own_ref.shape
    col, row = here_ref[0], here_ref[1]
    part = slice(LANES * unit, LANES * (unit + 1))
    mine = pl.ds(pl.multiple_of(lane + row * LANES, LANES), LANES)
    others = pl.ds(pl.multiple_of(lane + (1 - row) * LANES, LANES), LANES)
    for c in range(n_col):
        at = place_of(c ^ col, n_col)
        rows = slice(per * c, per * (c + 1))
        out[rows, mine] = own_ref[at, :, part]
        out[rows, others] = other_ref[at, :, part]


def first_kernel(size, here_ref, own_ref, other_ref, high_ref, low_ref, square, v):
    assemble(here_ref, own_ref, other_ref, 0, square, 0)
    inverse_of(square[...], v, high_ref, low_ref)


def half_scratch():
    return pltpu.VMEM((3, LANES // SUBS, SUBS, LANES), jnp.float32)


def first(size, here, own, other):
    shape = jax.ShapeDtypeStruct((size, size), HALF)
    return pl.pallas_call(
        functools.partial(first_kernel, size),
        in_specs=[SCALARS, ANY, ANY],
        out_specs=[ANY, ANY],
        out_shape=[shape, shape],
        scratch_shapes=[pltpu.VMEM((size, size), jnp.float32), half_scratch()],
        compiler_params=params(),
        cost_estimate=estimate(8),
        name="first",
    )(here, own, other)


def step_kernel(t, count, size, used, units, here_ref, *refs):
    raw = {}
    for k, name in enumerate(used):
        raw[name] = (refs[2 * k], refs[2 * k + 1])
    refs = refs[2 * len(used) :]
    inv = (refs[0], refs[1])
    past = [(refs[2 + 2 * i], refs[3 + 2 * i]) for i in range(t)]
    uh, ul, nh, nl, current, square, v = refs[2 + 2 * t :]
    blocks = count - 1 - t
    for k in range(blocks):
        name, unit = units[(t, t + 1 + k)]
        assemble(here_ref, *raw[name], unit, current, size * k)
    name, unit = units[(t + 1, t + 1)]
    assemble(here_ref, *raw[name], unit, square, 0)
    lefts = []
    for i in range(t):
        off = (t - 1 - i) * size
        lefts.append([ref[:, off : off + size].T for ref in past[i]])
    inverse = (inv[0][...], inv[1][...])
    for k in range(blocks):
        total = current[:, size * k : size * (k + 1)]
        for i in range(t):
            off = (t - i + k) * size
            right = [ref[:, off : off + size] for ref in past[i]]
            total = total - product(lefts[i], right, PLAIN)
        part = slice(size * k, size * (k + 1))
        uh[:, part], ul[:, part] = two(product(inverse, two(total), PLAIN))
    total = square[...]
    for i in range(t + 1):
        off = (t - i) * size
        pair = past[i] if i < t else (uh, ul)
        pair = [ref[:, off : off + size] for ref in pair]
        total = total - product([x.T for x in pair], pair, PLAIN)
    inverse_of(total, v, nh, nl)


def step(t, count, size, here, units, gathered, inv, past):
    used = sorted(
        {units[(t, u)][0] for u in range(t + 1, count)} | {units[(t + 1, t + 1)][0]}
    )
    flat = [x for name in used for x in gathered[name]]
    flat += list(inv) + [x for pair in past for x in pair]
    wide = jax.ShapeDtypeStruct((size, size * (count - 1 - t)), HALF)
    shape = jax.ShapeDtypeStruct((size, size), HALF)
    out = pl.pallas_call(
        functools.partial(step_kernel, t, count, size, used, units),
        in_specs=[SCALARS] + [ANY] * len(flat),
        out_specs=[ANY] * 4,
        out_shape=[wide, wide, shape, shape],
        scratch_shapes=[
            pltpu.VMEM(wide.shape, jnp.float32),
            pltpu.VMEM((size, size), jnp.float32),
            half_scratch(),
        ],
        compiler_params=params(),
        cost_estimate=estimate(12),
        name="step",
    )(here, *flat)
    return out[:2], out[2:]


def weights_kernel(count, size, here_ref, early_ref, late_ref, kept_ref, mine_ref, theirs_ref, *refs):
    inverses = [(refs[2 * t], refs[2 * t + 1]) for t in range(count)]
    refs = refs[2 * count :]
    past = [(refs[2 * t], refs[2 * t + 1]) for t in range(count - 1)]
    out_high, out_low, raw, wh, wl = refs[2 * (count - 1) :]
    n_col, per, lanes = early_ref.shape
    ahead = count // 2
    kept_here = lanes // ahead
    col, row = here_ref[0], here_ref[1]

    def block(t):
        return slice(t * size, (t + 1) * size)

    for t in range(count):
        for c in range(n_col):
            at = place_of(c ^ col, n_col)
            ref, k = (early_ref, t) if t < ahead else (late_ref, t - ahead)
            raw[per * c : per * (c + 1), :] = ref[
                at, :, kept_here * k : kept_here * (k + 1)
            ]
        z = raw[...].T
        for i in range(t):
            off = (t - 1 - i) * size
            right = [ref[:, off : off + size] for ref in past[i]]
            z = z - product((wh[:, block(i)], wl[:, block(i)]), right, PLAIN)
        z = product(two(z), [ref[...] for ref in inverses[t]], LAST)
        wh[:, block(t)], wl[:, block(t)] = two(z)
    for t in reversed(range(count)):
        z = wh[:, block(t)].astype(jnp.float32) + wl[:, block(t)].astype(jnp.float32)
        if t + 1 < count:
            later = slice((t + 1) * size, count * size)
            right = [ref[...] for ref in past[t]]
            z = z - product((wh[:, later], wl[:, later]), right, LAST)
        z = product(two(z), [ref[...] for ref in inverses[t]], PLAIN)
        wh[:, block(t)], wl[:, block(t)] = two(z)
    rows_here = kept_ref.shape[1]
    half = size // 2
    for side, hit_ref in ((0, mine_ref), (1, theirs_ref)):
        from_row = row if side == 0 else 1 - row
        for out, w in ((out_high, wh), (out_low, wl)):
            picked = jnp.concatenate(
                [
                    w[:, pl.ds(pl.multiple_of(t * size + from_row * half, half), half)]
                    for t in range(count)
                ],
                1,
            )
            spread = -mxu(picked, hit_ref[...], PLAIN)
            if side == 0 and out is out_high:
                spread = spread + kept_ref[...].astype(jnp.float32)
            out[:, side * rows_here : (side + 1) * rows_here] = spread.astype(HALF)


def weights(size, here, own, kept, mine, theirs, inverses, past):
    kept_here, rows_here = kept.shape
    count = len(inverses)
    flat = [x for pair in inverses for x in pair] + [x for pair in past for x in pair]
    shape = jax.ShapeDtypeStruct((kept_here, 2 * rows_here), HALF)
    return pl.pallas_call(
        functools.partial(weights_kernel, count, size),
        in_specs=[SCALARS] + [ANY] * (5 + len(flat)),
        out_specs=[ANY, ANY],
        out_shape=[shape, shape],
        scratch_shapes=[
            pltpu.VMEM((size, kept_here), jnp.float32),
            pltpu.VMEM((kept_here, count * size), HALF),
            pltpu.VMEM((kept_here, count * size), HALF),
        ],
        compiler_params=params(),
        cost_estimate=estimate(15),
        name="weights",
    )(here, *own, kept, mine, theirs, *flat)


def final_kernel(where_ref, high_ref, low_ref, mine_ref, theirs_ref, out_ref, result):
    rows_here, tile = mine_ref.shape
    kept_here = result.shape[0]
    out_ref[...] = jnp.zeros_like(out_ref)
    depth = 256
    total = None
    for side, ref in ((0, mine_ref), (1, theirs_ref)):
        for at in range(0, rows_here, depth):
            part = slice(side * rows_here + at, side * rows_here + at + depth)
            term = product(
                (high_ref[:, part], low_ref[:, part]),
                two(ref[at : at + depth, :]),
                PLAIN,
            )
            total = term if total is None else total + term
    result[...] = total

    def store(step, carry):
        base = pl.multiple_of(step * SUBS, SUBS)
        group = result[pl.ds(base, SUBS), :]
        for k in range(SUBS):
            out_ref[pl.ds(where_ref[base + k], 1), :] = group[k : k + 1, :]
        return carry

    lax.fori_loop(0, kept_here // SUBS, store, 0)


def final(where, high, low, mine, theirs):
    rows_here, cols = mine.shape
    tile = 512
    kept_here = high.shape[0]
    whole = pl.BlockSpec(high.shape, lambda i, w: (0, 0))
    strip = pl.BlockSpec((rows_here, tile), lambda i, w: (0, i))
    return pl.pallas_call(
        final_kernel,
        grid_spec=pltpu.PrefetchScalarGridSpec(
            num_scalar_prefetch=1,
            grid=(cols // tile,) if cols % tile == 0 else (pl.cdiv(cols, tile),),
            in_specs=[whole, whole, strip, strip],
            out_specs=strip,
            scratch_shapes=[pltpu.VMEM((kept_here, tile), jnp.float32)],
        ),
        out_shape=jax.ShapeDtypeStruct((rows_here, cols), jnp.float32),
        compiler_params=params(),
        cost_estimate=estimate(20),
        name="final",
    )(where, high, low, mine, theirs)


def plan(count, kept_units):
    full = count
    chunks = [
        [(0, 0, 1)],
        [(0, 1, full), (1, 1, 2)],
        [(1, 2, full), (2, 2, 3)],
        [(2, 3, full), (3, 3, 4)],
        [(3, 4, full), (4, 4, 5)],
        [(4, 5, full)] + [(t, t, full) for t in range(5, count)],
    ]
    units = {}
    for name, chunk in enumerate(chunks):
        at = 0
        for t, start, end in chunk:
            for u in range(start, end):
                units[(t, u)] = (name, at)
                at += 1
    for ts in (range(count // 2), range(count // 2, count)):
        chunks.append([(t, full, full + kept_units) for t in ts])
    return chunks, units


def per_device(slab, pivots):
    rows_here = slab.shape[0]
    n_col = lax.axis_size("col")
    n_row = lax.axis_size("row")
    col = lax.axis_index("col")
    row = lax.axis_index("row")
    lists, total = pivots.shape
    size = 256
    per = size // n_col
    pieces = total // size
    count = lists * pieces
    share = rows_here * n_row // n_col
    kept_here = rows_here - lists * total // n_row

    listed = pivots.reshape(lists, n_col, pieces, per)
    listed = jnp.transpose(listed, (0, 2, 1, 3)).reshape(count, n_col, per)
    own = lax.dynamic_index_in_dim(listed, col, 1, keepdims=False) - col * share
    own = own.reshape(count * per, 1)
    by_row = listed.reshape(count, n_row, size // n_row)
    mine = lax.dynamic_index_in_dim(by_row, row, 1, keepdims=False) - row * rows_here
    mine = mine.reshape(-1, 1)
    theirs = lax.dynamic_index_in_dim(by_row, 1 - row, 1, keepdims=False)
    theirs = theirs.reshape(-1, 1) - (1 - row) * rows_here
    theirs = (theirs == jnp.arange(rows_here, dtype=jnp.int32)[None]).astype(HALF)
    here = jnp.stack([col, row]).astype(jnp.int32)

    chunks, units = plan(count, kept_here // LANES)
    prepared = prepare(slab, own, mine, chunks, per, kept_here, share)
    kept, where, hit = prepared[-3:]
    where = where[:, 0]

    swap = [(0, 1), (1, 0)]
    raw = [x[None] for x in prepared[: len(chunks)]]
    far, near, gathered = {}, {}, {}

    def send_far(name):
        far[name] = [raw[name]] + [
            lax.ppermute(raw[name], "col", [(c, c ^ flip) for c in range(n_col)])
            for flip in range(2, n_col, 2)
        ]

    def send_near(name):
        held = jnp.concatenate(far[name], 0)
        near[name] = [
            held,
            lax.ppermute(held, "col", [(c, c ^ 1) for c in range(n_col)]),
        ]

    def send_across(name):
        held = jnp.concatenate(near[name], 0)
        gathered[name] = [held, lax.ppermute(held, "row", swap)]

    def tie(tables, token):
        flat, tree = jax.tree.flatten([tables, list(token)])
        return jax.tree.unflatten(tree, lax.optimization_barrier(flat))

    for name in (0, 1):
        send_far(name)
    send_near(0)
    send_far(2)
    send_across(0)
    send_far(3)
    send_near(1)
    inv = first(size, here, *gathered[0])
    (near[1], far[2], raw[4:]), inv = tie([near[1], far[2], raw[4:]], inv)
    send_near(2)
    for name in range(4, len(chunks)):
        send_far(name)
    send_across(1)
    inverses, past = [inv], []
    other_slab = None
    for t in range(count - 1):
        u, inv = step(t, count, size, here, units, gathered, inverses[t], past)
        if t < 4:
            (near[t + 2], far[t + 3]), inv = tie([near[t + 2], far[t + 3]], inv)
            send_near(t + 3)
            send_across(t + 2)
        elif t == 4:
            (near[6], far[7]), inv = tie([near[6], far[7]], inv)
            send_near(7)
        elif t == 5:
            (near[7],), inv = tie([near[7]], inv)
        if t == 1:
            (tied,), inv = tie([slab], inv)
            other_slab = lax.ppermute(tied, "row", swap)
        past.append(u)
        inverses.append(inv)
    kept_held = [jnp.concatenate(near[name], 0) for name in (6, 7)]
    high, low = weights(
        size, here, kept_held, kept, hit, theirs, inverses, past
    )
    return final(where, high, low, slab, other_slab)


def solution(mesh):
    in_specs = (P(("groups", "row"), "col"), P("groups", None))
    out_specs = P(("groups", "row"), "col")
    return jax.shard_map(
        per_device, mesh=mesh, in_specs=in_specs, out_specs=out_specs, check_vma=False
    )
```

```python
import functools

import jax
import jax.numpy as jnp
from jax import lax
from jax.experimental import pallas as pl
from jax.experimental.pallas import tpu as pltpu
from jax.sharding import PartitionSpec as P

LANES = 128
SUBS = 8
HALF = jnp.bfloat16
ANY = pl.BlockSpec(memory_space=pltpu.VMEM)
SCALARS = pl.BlockSpec(memory_space=pltpu.SMEM)
AHEAD = 3
VMEM_BYTES = 60 * 1024 * 1024

LEAD = (((0,), (0,)), ((), ()))
LAST = (((1,), (1,)), ((), ()))
PLAIN = (((1,), (0,)), ((), ()))


def mxu(left, right, dims):
    return lax.dot_general(left, right, dims, preferred_element_type=jnp.float32)


def two(x):
    high = x.astype(HALF)
    return high, (x - high.astype(jnp.float32)).astype(HALF)


def three(x):
    high = x.astype(HALF)
    rest = x - high.astype(jnp.float32)
    middle = rest.astype(HALF)
    return high, middle, (rest - middle.astype(jnp.float32)).astype(HALF)


def product(left, right, dims):
    rows = left[0].shape[0]
    both = mxu(jnp.concatenate(left, 0), right[0], dims)
    return both[:rows] + both[rows:] + mxu(left[0], right[1], dims)


def over_lanes(x, lane):
    return jnp.broadcast_to(x[:, lane : lane + 1], (SUBS, LANES))


def over_subs(x, sub):
    return jnp.broadcast_to(x[sub : sub + 1, :], (SUBS, LANES))


def gram(left, right):
    lh, lm, ll = three(left)
    rh, rm, rl = three(right)
    a = jnp.concatenate([lh, lm, lh, lm, ll, lh], 0)
    b = jnp.concatenate([rh, rh, rm, rm, rh, rl], 0)
    return mxu(a, b, LEAD)


def inverse_factor(v, order):
    wide = order // LANES
    panels = order // SUBS
    lane = lax.broadcasted_iota(jnp.int32, (SUBS, LANES), 1)
    sub = lax.broadcasted_iota(jnp.int32, (SUBS, LANES), 0)

    def load(q):
        return [v[q, :, LANES * c : LANES * (c + 1)] for c in range(wide)]

    def cleared(x, block, inside):
        return [jnp.where(inside, 0.0, x[c]) if c == block else x[c] for c in range(wide)]

    held = [load(q) for q in range(min(AHEAD, panels))]
    diag = [over_lanes(held[0][0], j) for j in range(SUBS)]
    for p in range(panels):
        block, first = SUBS * p // LANES, SUBS * p % LANES
        inside = (lane >= first) & (lane < first + SUBS)
        here = held[0]
        rows = [[over_subs(here[c], k) for c in range(wide)] for k in range(SUBS)]
        for k in range(SUBS):
            unit = jnp.where(lane == first + k, 1.0, 0.0)
            rows[k][block] = jnp.where(inside, unit, rows[k][block])
        coming = held[1:] + ([load(p + AHEAD)] if p + AHEAD < panels else [])
        entries = [[over_lanes(x[block], first + k) for k in range(SUBS)] for x in coming]
        if coming:
            nblock, nfirst = SUBS * (p + 1) // LANES, SUBS * (p + 1) % LANES
            ndiag = [over_lanes(coming[0][nblock], nfirst + k) for k in range(SUBS)]
        coming = [cleared(x, block, inside) for x in coming]
        packed = [None] * wide
        for k in range(SUBS):
            pivot = over_subs(diag[k], k)
            recip = 1.0 / pivot
            scale = lax.rsqrt(pivot)
            later = range(k + 1, SUBS)
            entry = {j: over_subs(diag[k], j) for j in later}
            column = diag[k] * recip
            for j in later:
                diag[j] = diag[j] - column * entry[j]
            for j in later:
                factor = entry[j] * recip
                for c in range(wide):
                    rows[j][c] = rows[j][c] - factor * rows[k][c]
            for a, (x, row) in enumerate(zip(entries, coming)):
                column = x[k] * recip
                for j in later:
                    x[j] = x[j] - column * entry[j]
                if a == 0:
                    for i in range(SUBS):
                        ndiag[i] = ndiag[i] - x[k] * over_subs(column, i)
                for c in range(wide):
                    row[c] = row[c] - column * rows[k][c]
            for c in range(wide):
                row = rows[k][c] * scale
                packed[c] = row if k == 0 else jnp.where(sub == k, row, packed[c])
        for c in range(wide):
            v[p, :, LANES * c : LANES * (c + 1)] = packed[c]
        if coming:
            diag, held = ndiag, coming
        if p + AHEAD + 1 < panels:
            start = SUBS * (p + AHEAD + 1) // LANES
            change = gram(jnp.concatenate(packed[start:], 1), jnp.concatenate(packed, 1))
            for q in range(p + AHEAD + 1, panels):
                at = SUBS * q - LANES * start
                for c in range(wide):
                    old = v[q, :, LANES * c : LANES * (c + 1)]
                    if c == block:
                        old = jnp.where(inside, 0.0, old)
                    new = change[at : at + SUBS, LANES * c : LANES * (c + 1)]
                    v[q, :, LANES * c : LANES * (c + 1)] = old - new


def params():
    return pltpu.CompilerParams(vmem_limit_bytes=VMEM_BYTES)


def estimate(microseconds):
    return pl.CostEstimate(
        flops=microseconds * 1_000_000_000, bytes_accessed=1_000_000, transcendentals=0
    )


def exact(left, right, dims):
    return lax.dot_general(
        left,
        right,
        dims,
        precision=lax.Precision.HIGHEST,
        preferred_element_type=jnp.float32,
    )


def inverse_of(square, v, high_ref, low_ref):
    n = LANES
    v[0] = square[:n, :n].reshape(n // SUBS, SUBS, n)
    above = square[:n, n:]
    last = square[n:, n:]
    down = lax.broadcasted_iota(jnp.int32, (n, n), 0)
    across = lax.broadcasted_iota(jnp.int32, (n, n), 1)

    def half(h, carry):
        inverse_factor(v.at[h], n)
        done = jnp.where(across <= down, v[h].reshape(n, n), 0.0)
        v[h] = done.reshape(n // SUBS, SUBS, n)

        @pl.when(h == 0)
        def _():
            upper = exact(done, above, PLAIN)
            v[2] = upper.reshape(n // SUBS, SUBS, n)
            v[1] = (last - exact(upper, upper, LEAD)).reshape(n // SUBS, SUBS, n)

        return carry

    lax.fori_loop(0, 2, half, 0)
    first, second, upper = (v[h].reshape(n, n) for h in range(3))
    corner = -exact(second, exact(upper, first, LEAD), PLAIN)
    zero = jnp.zeros((n, n), HALF)
    for at, piece in (((0, 0), first), ((n, 0), corner), ((n, n), second)):
        block = (slice(at[0], at[0] + n), slice(at[1], at[1] + n))
        high_ref[block], low_ref[block] = two(piece)
    high_ref[:n, n:] = zero
    low_ref[:n, n:] = zero


def prepare_kernel(chunks, per, kept_here, slab_ref, own_ref, rows_ref, *outs):
    rows_here, width = slab_ref.shape
    picks = own_ref.shape[0]
    listed = rows_ref.shape[0]
    pieces, (kept_ref, where_ref, hit_ref) = outs[:-3], outs[-3:]
    f32 = jnp.float32
    column = lax.broadcasted_iota(jnp.int32, (picks, width), 1)
    choose = jnp.where(own_ref[...] == column, 1.0, 0.0).astype(HALF)
    row = lax.broadcasted_iota(jnp.int32, (listed, rows_here), 1)
    hit = jnp.where(rows_ref[...] == row, 1.0, 0.0)
    kept = 1.0 - jnp.sum(hit, axis=0, keepdims=True)
    hit = hit.astype(HALF)
    hit_ref[...] = hit
    before = lax.broadcasted_iota(jnp.int32, (rows_here, rows_here), 0) < (
        lax.broadcasted_iota(jnp.int32, (rows_here, rows_here), 1)
    )
    before = jnp.where(before, 1.0, 0.0).astype(HALF)
    rank = mxu(jnp.broadcast_to(kept, (SUBS, rows_here)).astype(HALF), before, PLAIN)
    place = lax.broadcasted_iota(jnp.int32, (kept_here, rows_here), 0).astype(f32)
    hit_kept = jnp.where((rank[0:1, :] == place) & (kept > 0.5), 1.0, 0.0)
    number = lax.broadcasted_iota(jnp.int32, (kept_here, rows_here), 1).astype(f32)
    where_ref[...] = jnp.broadcast_to(
        jnp.sum(hit_kept * number, axis=1, keepdims=True), where_ref.shape
    ).astype(jnp.int32)
    hit_kept = hit_kept.astype(HALF)
    kept_ref[...] = hit_kept
    order = jnp.concatenate([hit, hit_kept], 0)
    total = None
    for piece in three(slab_ref[...]):
        chosen = mxu(choose, piece, LAST).astype(HALF)
        part = mxu(chosen, order, LAST)
        total = part if total is None else total + part
    for out, chunk in zip(pieces, chunks):
        at = 0
        for t, start, end in chunk:
            wide = LANES * (end - start)
            out[:, at : at + wide] = total[
                per * t : per * (t + 1), LANES * start : LANES * end
            ]
            at += wide


def prepare(slab, own, rows, chunks, per, kept_here, share):
    rows_here = slab.shape[0]
    width = -(-share // LANES) * LANES
    f32 = jnp.float32
    shapes = [
        jax.ShapeDtypeStruct((per, LANES * sum(e - s for _, s, e in chunk)), f32)
        for chunk in chunks
    ]
    shapes.append(jax.ShapeDtypeStruct((kept_here, rows_here), HALF))
    shapes.append(jax.ShapeDtypeStruct((kept_here, LANES), jnp.int32))
    shapes.append(jax.ShapeDtypeStruct((rows.shape[0], rows_here), HALF))
    return pl.pallas_call(
        functools.partial(prepare_kernel, chunks, per, kept_here),
        grid=(1,),
        in_specs=[
            pl.BlockSpec((rows_here, width), lambda i: (0, 0)),
            pl.BlockSpec(own.shape, lambda i: (0, 0)),
            pl.BlockSpec(rows.shape, lambda i: (0, 0)),
        ],
        out_specs=[pl.BlockSpec(s.shape, lambda i: (0, 0)) for s in shapes],
        out_shape=shapes,
        compiler_params=params(),
        cost_estimate=estimate(7),
        name="prepare",
    )(slab, own, rows)


def place_of(flipped, n_col):
    return (flipped & 1) * (n_col // 2) + (flipped >> 1)


def assemble(here_ref, own_ref, other_ref, unit, out, lane):
    n_col, per, _ = own_ref.shape
    col, row = here_ref[0], here_ref[1]
    part = slice(LANES * unit, LANES * (unit + 1))
    mine = pl.ds(pl.multiple_of(lane + row * LANES, LANES), LANES)
    others = pl.ds(pl.multiple_of(lane + (1 - row) * LANES, LANES), LANES)
    for c in range(n_col):
        at = place_of(c ^ col, n_col)
        rows = slice(per * c, per * (c + 1))
        out[rows, mine] = own_ref[at, :, part]
        out[rows, others] = other_ref[at, :, part]


def first_kernel(size, here_ref, own_ref, other_ref, high_ref, low_ref, square, v):
    assemble(here_ref, own_ref, other_ref, 0, square, 0)
    inverse_of(square[...], v, high_ref, low_ref)


def half_scratch():
    return pltpu.VMEM((3, LANES // SUBS, SUBS, LANES), jnp.float32)


def first(size, here, own, other):
    shape = jax.ShapeDtypeStruct((size, size), HALF)
    return pl.pallas_call(
        functools.partial(first_kernel, size),
        in_specs=[SCALARS, ANY, ANY],
        out_specs=[ANY, ANY],
        out_shape=[shape, shape],
        scratch_shapes=[pltpu.VMEM((size, size), jnp.float32), half_scratch()],
        compiler_params=params(),
        cost_estimate=estimate(8),
        name="first",
    )(here, own, other)


def step_kernel(t, count, size, used, units, here_ref, *refs):
    raw = {}
    for k, name in enumerate(used):
        raw[name] = (refs[2 * k], refs[2 * k + 1])
    refs = refs[2 * len(used) :]
    inv = (refs[0], refs[1])
    past = [(refs[2 + 2 * i], refs[3 + 2 * i]) for i in range(t)]
    uh, ul, nh, nl, current, square, v = refs[2 + 2 * t :]
    blocks = count - 1 - t
    for k in range(blocks):
        name, unit = units[(t, t + 1 + k)]
        assemble(here_ref, *raw[name], unit, current, size * k)
    name, unit = units[(t + 1, t + 1)]
    assemble(here_ref, *raw[name], unit, square, 0)
    lefts = []
    for i in range(t):
        off = (t - 1 - i) * size
        lefts.append([ref[:, off : off + size].T for ref in past[i]])
    inverse = (inv[0][...], inv[1][...])
    for k in range(blocks):
        total = current[:, size * k : size * (k + 1)]
        for i in range(t):
            off = (t - i + k) * size
            right = [ref[:, off : off + size] for ref in past[i]]
            total = total - product(lefts[i], right, PLAIN)
        part = slice(size * k, size * (k + 1))
        uh[:, part], ul[:, part] = two(product(inverse, two(total), PLAIN))
    total = square[...]
    for i in range(t + 1):
        off = (t - i) * size
        pair = past[i] if i < t else (uh, ul)
        pair = [ref[:, off : off + size] for ref in pair]
        total = total - product([x.T for x in pair], pair, PLAIN)
    inverse_of(total, v, nh, nl)


def step(t, count, size, here, units, gathered, inv, past):
    used = sorted(
        {units[(t, u)][0] for u in range(t + 1, count)} | {units[(t + 1, t + 1)][0]}
    )
    flat = [x for name in used for x in gathered[name]]
    flat += list(inv) + [x for pair in past for x in pair]
    wide = jax.ShapeDtypeStruct((size, size * (count - 1 - t)), HALF)
    shape = jax.ShapeDtypeStruct((size, size), HALF)
    out = pl.pallas_call(
        functools.partial(step_kernel, t, count, size, used, units),
        in_specs=[SCALARS] + [ANY] * len(flat),
        out_specs=[ANY] * 4,
        out_shape=[wide, wide, shape, shape],
        scratch_shapes=[
            pltpu.VMEM(wide.shape, jnp.float32),
            pltpu.VMEM((size, size), jnp.float32),
            half_scratch(),
        ],
        compiler_params=params(),
        cost_estimate=estimate(12),
        name="step",
    )(here, *flat)
    return out[:2], out[2:]


def weights_kernel(count, size, here_ref, early_ref, late_ref, kept_ref, mine_ref, theirs_ref, *refs):
    inverses = [(refs[2 * t], refs[2 * t + 1]) for t in range(count)]
    refs = refs[2 * count :]
    past = [(refs[2 * t], refs[2 * t + 1]) for t in range(count - 1)]
    out_high, out_low, raw, wh, wl = refs[2 * (count - 1) :]
    n_col, per, lanes = early_ref.shape
    ahead = count // 2
    kept_here = lanes // ahead
    col, row = here_ref[0], here_ref[1]

    def block(t):
        return slice(t * size, (t + 1) * size)

    for t in range(count):
        for c in range(n_col):
            at = place_of(c ^ col, n_col)
            ref, k = (early_ref, t) if t < ahead else (late_ref, t - ahead)
            raw[per * c : per * (c + 1), :] = ref[
                at, :, kept_here * k : kept_here * (k + 1)
            ]
        z = raw[...].T
        for i in range(t):
            off = (t - 1 - i) * size
            right = [ref[:, off : off + size] for ref in past[i]]
            z = z - product((wh[:, block(i)], wl[:, block(i)]), right, PLAIN)
        z = product(two(z), [ref[...] for ref in inverses[t]], LAST)
        wh[:, block(t)], wl[:, block(t)] = two(z)
    for t in reversed(range(count)):
        z = wh[:, block(t)].astype(jnp.float32) + wl[:, block(t)].astype(jnp.float32)
        if t + 1 < count:
            later = slice((t + 1) * size, count * size)
            right = [ref[...] for ref in past[t]]
            z = z - product((wh[:, later], wl[:, later]), right, LAST)
        z = product(two(z), [ref[...] for ref in inverses[t]], PLAIN)
        wh[:, block(t)], wl[:, block(t)] = two(z)
    rows_here = kept_ref.shape[1]
    half = size // 2
    for side, hit_ref in ((0, mine_ref), (1, theirs_ref)):
        from_row = row if side == 0 else 1 - row
        for out, w in ((out_high, wh), (out_low, wl)):
            picked = jnp.concatenate(
                [
                    w[:, pl.ds(pl.multiple_of(t * size + from_row * half, half), half)]
                    for t in range(count)
                ],
                1,
            )
            spread = -mxu(picked, hit_ref[...], PLAIN)
            if side == 0 and out is out_high:
                spread = spread + kept_ref[...].astype(jnp.float32)
            out[:, side * rows_here : (side + 1) * rows_here] = spread.astype(HALF)


def weights(size, here, own, kept, mine, theirs, inverses, past):
    kept_here, rows_here = kept.shape
    count = len(inverses)
    flat = [x for pair in inverses for x in pair] + [x for pair in past for x in pair]
    shape = jax.ShapeDtypeStruct((kept_here, 2 * rows_here), HALF)
    return pl.pallas_call(
        functools.partial(weights_kernel, count, size),
        in_specs=[SCALARS] + [ANY] * (5 + len(flat)),
        out_specs=[ANY, ANY],
        out_shape=[shape, shape],
        scratch_shapes=[
            pltpu.VMEM((size, kept_here), jnp.float32),
            pltpu.VMEM((kept_here, count * size), HALF),
            pltpu.VMEM((kept_here, count * size), HALF),
        ],
        compiler_params=params(),
        cost_estimate=estimate(15),
        name="weights",
    )(here, *own, kept, mine, theirs, *flat)


def final_kernel(where_ref, high_ref, low_ref, mine_ref, theirs_ref, out_ref, result):
    rows_here, tile = mine_ref.shape
    kept_here = result.shape[0]
    out_ref[...] = jnp.zeros_like(out_ref)
    depth = 256
    total = None
    for side, ref in ((0, mine_ref), (1, theirs_ref)):
        for at in range(0, rows_here, depth):
            part = slice(side * rows_here + at, side * rows_here + at + depth)
            term = product(
                (high_ref[:, part], low_ref[:, part]),
                two(ref[at : at + depth, :]),
                PLAIN,
            )
            total = term if total is None else total + term
    result[...] = total

    def store(step, carry):
        base = pl.multiple_of(step * SUBS, SUBS)
        group = result[pl.ds(base, SUBS), :]
        for k in range(SUBS):
            out_ref[pl.ds(where_ref[base + k], 1), :] = group[k : k + 1, :]
        return carry

    lax.fori_loop(0, kept_here // SUBS, store, 0)


def final(where, high, low, mine, theirs):
    rows_here, cols = mine.shape
    tile = next(x for x in (896, 512, 256, 128) if cols % x == 0)
    kept_here = high.shape[0]
    whole = pl.BlockSpec(high.shape, lambda i, w: (0, 0))
    strip = pl.BlockSpec((rows_here, tile), lambda i, w: (0, i))
    return pl.pallas_call(
        final_kernel,
        grid_spec=pltpu.PrefetchScalarGridSpec(
            num_scalar_prefetch=1,
            grid=(cols // tile,),
            in_specs=[whole, whole, strip, strip],
            out_specs=strip,
            scratch_shapes=[pltpu.VMEM((kept_here, tile), jnp.float32)],
        ),
        out_shape=jax.ShapeDtypeStruct((rows_here, cols), jnp.float32),
        compiler_params=params(),
        cost_estimate=estimate(20),
        name="final",
    )(where, high, low, mine, theirs)


def plan(count, kept_units):
    full = count
    chunks = [
        [(0, 0, 1)],
        [(0, 1, full), (1, 1, 2)],
        [(1, 2, full), (2, 2, 3)],
        [(2, 3, full), (3, 3, 4)],
        [(3, 4, full), (4, 4, 5)],
        [(4, 5, full)] + [(t, t, full) for t in range(5, count)],
    ]
    units = {}
    for name, chunk in enumerate(chunks):
        at = 0
        for t, start, end in chunk:
            for u in range(start, end):
                units[(t, u)] = (name, at)
                at += 1
    for ts in (range(count // 2), range(count // 2, count)):
        chunks.append([(t, full, full + kept_units) for t in ts])
    return chunks, units


def per_device(slab, pivots):
    rows_here = slab.shape[0]
    n_col = lax.axis_size("col")
    n_row = lax.axis_size("row")
    col = lax.axis_index("col")
    row = lax.axis_index("row")
    lists, total = pivots.shape
    size = 256
    per = size // n_col
    pieces = total // size
    count = lists * pieces
    share = rows_here * n_row // n_col
    kept_here = rows_here - lists * total // n_row

    listed = pivots.reshape(lists, n_col, pieces, per)
    listed = jnp.transpose(listed, (0, 2, 1, 3)).reshape(count, n_col, per)
    own = lax.dynamic_index_in_dim(listed, col, 1, keepdims=False) - col * share
    own = own.reshape(count * per, 1)
    by_row = listed.reshape(count, n_row, size // n_row)
    mine = lax.dynamic_index_in_dim(by_row, row, 1, keepdims=False) - row * rows_here
    mine = mine.reshape(-1, 1)
    theirs = lax.dynamic_index_in_dim(by_row, 1 - row, 1, keepdims=False)
    theirs = theirs.reshape(-1, 1) - (1 - row) * rows_here
    theirs = (theirs == jnp.arange(rows_here, dtype=jnp.int32)[None]).astype(HALF)
    here = jnp.stack([col, row]).astype(jnp.int32)

    chunks, units = plan(count, kept_here // LANES)
    carriers = [(0,), (1,), (2, 3), (4,), (5,), (6,), (7,)]
    carried = [sum((chunks[name] for name in names), []) for names in carriers]
    prepared = prepare(slab, own, mine, carried, per, kept_here, share)
    spans = {}
    for k, names in enumerate(carriers):
        at = 0
        for name in names:
            wide = LANES * sum(end - start for _, start, end in chunks[name])
            spans[name] = (k, at, at + wide)
            at += wide
    kept, where, hit = prepared[-3:]
    where = where[:, 0]

    swap = [(0, 1), (1, 0)]
    raw = [x[None] for x in prepared[: len(carriers)]]
    far, near, gathered = {}, {}, {}

    def send_far(name):
        far[name] = [raw[name]] + [
            lax.ppermute(raw[name], "col", [(c, c ^ flip) for c in range(n_col)])
            for flip in range(2, n_col, 2)
        ]

    def send_near(name):
        k, start, end = spans[name]
        held = jnp.concatenate([x[:, :, start:end] for x in far[k]], 0)
        near[name] = [
            held,
            lax.ppermute(held, "col", [(c, c ^ 1) for c in range(n_col)]),
        ]

    def send_across(name):
        held = jnp.concatenate(near[name], 0)
        gathered[name] = [held, lax.ppermute(held, "row", swap)]

    def tie(tables, token):
        flat, tree = jax.tree.flatten([tables, list(token)])
        return jax.tree.unflatten(tree, lax.optimization_barrier(flat))

    for k in (0, 1):
        send_far(k)
    send_near(0)
    send_far(2)
    send_across(0)
    send_near(1)
    inv = first(size, here, *gathered[0])
    (near[1], far[2], raw[3:]), inv = tie([near[1], far[2], raw[3:]], inv)
    send_near(2)
    send_far(3)
    send_across(1)
    inverses, past = [inv], []
    for t in range(count - 1):
        u, inv = step(t, count, size, here, units, gathered, inverses[t], past)
        if t < 4:
            (near[t + 2], far[t + 2], raw[t + 4 :]), inv = tie(
                [near[t + 2], far[t + 2], raw[t + 4 :]], inv
            )
            send_near(t + 3)
            send_across(t + 2)
            if t < 3:
                send_far(t + 4)
        elif t == 4:
            (near[6], far[6]), inv = tie([near[6], far[6]], inv)
            send_near(7)
        elif t == 5:
            (near[7],), inv = tie([near[7]], inv)
        if t == 1:
            (tied,), inv = tie([slab], inv)
            other_slab = lax.ppermute(tied, "row", swap)
        past.append(u)
        inverses.append(inv)
    kept_held = [jnp.concatenate(near[name], 0) for name in (6, 7)]
    high, low = weights(
        size, here, kept_held, kept, hit, theirs, inverses, past
    )
    return final(where, high, low, slab, other_slab)


def solution(mesh):
    in_specs = (P(("groups", "row"), "col"), P("groups", None))
    out_specs = P(("groups", "row"), "col")
    return jax.shard_map(
        per_device, mesh=mesh, in_specs=in_specs, out_specs=out_specs, check_vma=False
    )
```
